512 devices in a mesh: ctx: 64 (over z_lo, x, core), tp: 8 (over y, z_hi).
Axes of the slice: x: 4, y: 4, z: 16 (z_hi: 2, z_lo: 8; z = z_hi * 8 + z_lo), core: 2. Of those that a mesh axis runs over, the one named last changes fastest.
Arguments:
- hidden_x: bfloat16 [8192, 8192], P('ctx', 'tp'), may hold values from -100 to 100, as said below
- norm_gain: float32 [8192], replicated, may hold values from 0.1 to 1.9
- key_projection: bfloat16 [8192, 1024], P('ctx', 'tp'), may hold values from -0.0625 to 0.0625
- value_projection: bfloat16 [8192, 1024], P('ctx', 'tp'), may hold values from -0.0625 to 0.0625
- queries: bfloat16 [8192, 8192], P('ctx', 'tp'), may hold values from -160 to 160
- span_pair: int32 [64], P('ctx'), may hold values from 0 to 63, each once
- doc_lengths: int32 [12], replicated, may hold values from 1 to 2048, 8192 in all
Outputs:
- attended: bfloat16 [8192, 8192], P('ctx', 'tp')
The draws below stay inside these ranges and needn't reach their ends.
Inputs may be any that keep to these rules, and one draw needn't show every extreme that they name: `hidden_x`: hidden states of tokens and features of different scales. `span_pair`: each pair index is held by exactly one index of ctx. `doc_lengths`: they sum to 8192; the longest has 2048 tokens.
All inputs are finite; a program needn't handle non-finite values.
Results may differ from the reference program's by a relative error of at most 0.0078.
Values may be sent and summed in bfloat16 or wider, within the bound.
A program may use at most 128 MiB of HBM per device.

```python
import math
import jax
import jax.numpy as jnp
import numpy as np
from jax import lax

MODEL_WIDTH = 8192
QUERY_HEADS = 64
KEY_VALUE_HEADS = 8
HEAD_SIZE = 128
TOK_DEV = 128
DOCS = 12
HALF = 64
SEQUENCE_TOKENS = 8192
DOC_MOST = 2048
N_CTX = 64


def draw_hidden_x(key, part):
    first_key, second_key, third_key = jax.random.split(key, 3)
    row_scale = jnp.exp(jax.random.uniform(second_key, (SEQUENCE_TOKENS, 1), jnp.float32, math.log(0.5), math.log(5.0)))
    column_scale = jnp.exp(jax.random.uniform(third_key, (1, MODEL_WIDTH), jnp.float32, math.log(0.3), math.log(3.0)))
    base_draw = jax.random.normal(first_key, (SEQUENCE_TOKENS, MODEL_WIDTH), jnp.float32)
    return jnp.clip(base_draw * row_scale * column_scale, -100.0, 100.0).astype(jnp.bfloat16)


def draw_queries(key, part):
    first_key = jax.random.fold_in(key, 0)
    base_draw = jnp.clip(1.5 * jax.random.normal(first_key, (SEQUENCE_TOKENS, QUERY_HEADS * HEAD_SIZE), jnp.float32), -9.0, 9.0)
    return jnp.clip(base_draw, -160.0, 160.0).astype(jnp.bfloat16)


def levels(rng, dims, cuts, least, high):
    level = 1.0
    for position, blocks in cuts:
        draws = jax.random.uniform(jax.random.fold_in(jax.random.fold_in(rng, 6), position), (blocks,), jnp.float32, least / len(cuts), high / len(cuts))
        level = level * jnp.repeat(jnp.exp(draws), dims[position] // blocks).reshape((-1,) + (1,) * (len(dims) - 1 - position))
    return level


def profile(count, total, bound, slope):
    loads = [(1 << 20) // math.isqrt(standing ** slope) + 1 for standing in range(2, count + 1)]
    spare, counts = total - bound - (count - 1), [1] * (count - 1)
    while spare > 0:
        candidates = [i for i in range(count - 1) if counts[i] < bound]
        mass, remaining = sum([loads[i] for i in candidates]), spare
        for i in candidates:
            addition = min(bound - counts[i], max(1, remaining * loads[i] // mass), spare)
            counts[i] = counts[i] + addition
            spare = spare - addition
    return np.array([bound] + counts)


def uneven(stream_key, number_of, total, most, skew):
    if number_of == 2:
        one = jax.random.randint(stream_key, (), max(1, total - most), min(most, total - 1) + 1)
        return jnp.stack([one, total - one])
    lengths = jnp.asarray(profile(number_of, total, most, skew), jnp.int32)
    pairs = (number_of - 1) // 2
    donor, sink = lengths[1:1 + 2 * pairs:2], lengths[2:2 + 2 * pairs:2]
    room = jnp.minimum(donor - 1, most - sink)
    moved = jax.random.randint(jax.random.fold_in(stream_key, 1), (pairs,), 0, 1 << 20) % (room + 1)
    lengths = lengths.at[1:1 + 2 * pairs:2].set(donor - moved).at[2:2 + 2 * pairs:2].set(sink + moved)
    return lengths[jax.random.permutation(jax.random.fold_in(stream_key, 2), number_of)]


def normal_values(key, extent, scale, reach, cuts=(), kind=jnp.bfloat16):
    loudness = levels(key, extent, cuts, -0.22, 0.18) if cuts else 1.0
    values = jax.random.normal(key, extent, jnp.float32) * scale * loudness
    return jnp.minimum(jnp.maximum(values, -reach), reach).astype(kind)


def setup_inputs(seed: int = 0) -> dict:
    key_list = jax.random.split(jax.random.key(seed), 8)
    return {
        "hidden_x": draw_hidden_x(jax.random.fold_in(key_list[7], 71), 0),
        "norm_gain": jnp.clip(1.0 + 0.18 * jax.random.normal(key_list[1], (MODEL_WIDTH,), jnp.float32), 0.1, 1.9),
        "key_projection": normal_values(key_list[2], (MODEL_WIDTH, KEY_VALUE_HEADS * HEAD_SIZE), MODEL_WIDTH ** -0.5, 0.0625, ((0, 64), (1, 8))),
        "value_projection": normal_values(key_list[3], (MODEL_WIDTH, KEY_VALUE_HEADS * HEAD_SIZE), MODEL_WIDTH ** -0.5, 0.0625, ((0, 64), (1, 8))),
        "queries": draw_queries(jax.random.fold_in(key_list[7], 71), 0),
        "span_pair": jax.random.permutation(key_list[5], N_CTX).astype(jnp.int32),
        "doc_lengths": uneven(key_list[6], DOCS, SEQUENCE_TOKENS, DOC_MOST, 2).astype(jnp.int32),
    }


ROPE_BASE = 500000.0
EPSILON = 1e-05
NEG_BIG = -1e+30

def rotate_heads(raw, positions, head_dim):
    tokens_here = raw.shape[0]
    heads_here = raw.shape[1] // head_dim
    half_dim = head_dim // 2
    split_heads = raw.reshape(tokens_here, heads_here, head_dim)
    exponents = jnp.arange(half_dim, dtype=jnp.float32) * (2.0 / head_dim)
    inverse = jnp.power(jnp.float32(ROPE_BASE), -exponents)
    angles = positions.astype(jnp.float32)[:, None] * inverse[None, :]
    cosine = jnp.cos(angles)[:, None, :]
    sine_part = jnp.sin(angles)[:, None, :]
    first_half = split_heads[..., :half_dim]
    second_half = split_heads[..., half_dim:]
    turned = jnp.concatenate([first_half * cosine - second_half * sine_part, second_half * cosine + first_half * sine_part], axis=-1)
    return turned.reshape(tokens_here, heads_here * head_dim)

def place_tokens(pair_of_token, offsets, half_rows, span_total):
    early = pair_of_token * half_rows + offsets
    late = (span_total - 1 - pair_of_token) * half_rows + offsets - half_rows
    return jnp.where(offsets < half_rows, early, late).astype(jnp.int32)

def document_of(positions, doc_ends):
    return lax.optimization_barrier(jnp.sum((positions[:, None] >= doc_ends[None, :]).astype(jnp.int32), axis=1)).astype(jnp.int32)

def normalize(hidden_x, norm_gain):
    widened = hidden_x.astype(jnp.float32)
    mean_square = lax.optimization_barrier(jnp.mean(widened * widened, axis=-1, keepdims=True))
    return (widened * lax.rsqrt(mean_square + EPSILON) * norm_gain).astype(jnp.bfloat16)

def reference(hidden_x, norm_gain, key_projection, value_projection, queries, span_pair, doc_lengths):
    token_ids = jnp.arange(SEQUENCE_TOKENS, dtype=jnp.int32)
    owners = token_ids // TOK_DEV
    offsets = token_ids % TOK_DEV
    positions = place_tokens(span_pair[owners], offsets, HALF, 2 * N_CTX)
    doc_ends = jnp.cumsum(doc_lengths).astype(jnp.int32)
    documents = document_of(positions, doc_ends)
    normed = normalize(hidden_x, norm_gain)
    key_raw = jnp.dot(normed, key_projection, preferred_element_type=jnp.float32)
    value_raw = jnp.dot(normed, value_projection, preferred_element_type=jnp.float32)
    rows_of_key = rotate_heads(key_raw, positions, HEAD_SIZE).astype(jnp.bfloat16)
    rows_of_value = value_raw.astype(jnp.bfloat16)
    group_width = QUERY_HEADS // KEY_VALUE_HEADS
    heads_of_key = rows_of_key.astype(jnp.float32).reshape(SEQUENCE_TOKENS, KEY_VALUE_HEADS, HEAD_SIZE).transpose(1, 0, 2)
    heads_of_value = rows_of_value.astype(jnp.float32).reshape(SEQUENCE_TOKENS, KEY_VALUE_HEADS, HEAD_SIZE).transpose(1, 0, 2)
    block_rows = math.gcd(SEQUENCE_TOKENS, 512)
    block_count = SEQUENCE_TOKENS // block_rows
    query_blocks = queries.astype(jnp.float32).reshape(block_count, block_rows, QUERY_HEADS, HEAD_SIZE).transpose(0, 2, 1, 3)
    position_blocks = positions.reshape(block_count, block_rows)
    document_blocks = documents.reshape(block_count, block_rows)
    head_ids = jnp.arange(QUERY_HEADS, dtype=jnp.int32)
    scale_factor = HEAD_SIZE ** (-0.5)

    def one_block(block_inputs):
        query_block, block_positions, block_documents = block_inputs
        allowed = (documents[None, :] == block_documents[:, None]) & (positions[None, :] <= block_positions[:, None])

        def one_head(head_inputs):
            query_one, head_id = head_inputs
            shared_head = head_id // group_width
            key_one = heads_of_key[shared_head]
            value_one = heads_of_value[shared_head]
            scores = jnp.dot(query_one, key_one.T, preferred_element_type=jnp.float32) * scale_factor
            scores = jnp.where(allowed, scores, NEG_BIG)
            row_top = lax.optimization_barrier(jnp.max(scores, axis=1, keepdims=True))
            exp_scores = jnp.where(allowed, jnp.exp(scores - row_top), 0.0)
            denominator = lax.optimization_barrier(jnp.sum(exp_scores, axis=1, keepdims=True))
            rounded = lax.optimization_barrier(exp_scores.astype(jnp.bfloat16))
            summed = jnp.dot(rounded.astype(jnp.float32), value_one, preferred_element_type=jnp.float32)
            return (summed / denominator).astype(jnp.bfloat16)
        return lax.map(one_head, (query_block, head_ids))
    outputs = lax.map(one_block, (query_blocks, position_blocks, document_blocks))
    return outputs.transpose(0, 2, 1, 3).reshape(SEQUENCE_TOKENS, QUERY_HEADS * HEAD_SIZE)
```

```python
import functools
import math

import jax
import jax.numpy as jnp
import numpy as np
from jax import lax
from jax.experimental import pallas as pl
from jax.experimental.pallas import tpu as pltpu
from jax.sharding import PartitionSpec as P

HEAD = 128
ROPE_BASE = 500000.0
EPSILON = 1e-05
NEG = -1e30
MESH = pl.DeviceIdType.MESH
NZ, NX, NY = 8, 4, 4
NCTX = NZ * NX * 2
HALF = 64
EXT = 16
VMEM_LIMIT = 60 * 1024 * 1024
HUB = {0: (4, 1), 1: (2,), 2: (3,), 4: (6, 5), 6: (7,)}
LINE = {i: (i + 1,) for i in range(NZ - 1)}
SPREAD = (
    "z0", "z1", "z4", "z2", "x0", "z5", "z3", "x1", "z6", "a0", "x4", "z7", "x2", "a1", "x5", "a4", "x3", "a2", "x6",
    "a5", "x7", "a3", "a6", "a7",
)
REACHES = (1, 2, 4)


def block_id(z, x, k):
    return z * (NX * 2) + x * 2 + k


class Place:
    def __init__(self):
        self.ctx = lax.axis_index("ctx")
        self.tp = lax.axis_index("tp")
        self.z = self.ctx // (NX * 2)
        self.x = (self.ctx // 2) % NX
        self.k = self.ctx % 2
        self.y = self.tp // 2
        self.h = self.tp % 2

    def ctx_neighbour(self, what):
        if isinstance(what, int):
            return block_id(self.z + what, self.x, self.k)
        if what == "right":
            return block_id(self.z, (self.x + 1) % NX, self.k)
        if what == "left":
            return block_id(self.z, (self.x + NX - 1) % NX, self.k)
        return block_id(self.z, self.x, 1 - self.k)


def copy_to(src, dst, send, recv, device):
    return pltpu.make_async_remote_copy(
        src_ref=src, dst_ref=dst, send_sem=send, recv_sem=recv, device_id=device, device_id_type=MESH
    )


class CtxGather:
    def __init__(self, place, tree, bufs, send, recv):
        self.p, self.tree, self.bufs, self.send, self.recv = place, tree, bufs, send, recv

    N_SEND = 74

    def copy(self, array, block, slot, way):
        ref = self.bufs[array].at[block]
        return copy_to(
            ref,
            ref,
            self.send.at[array, slot],
            self.recv.at[array, block],
            {"ctx": self.p.ctx_neighbour(way)},
        )

    def arrived(self, array, block):
        self.copy(array, block, 0, "core").wait_recv()

    def spread(self, array, zb):
        p = self.p
        own = block_id(zb, p.x, p.k)
        self.copy(array, own, 18 + zb, "right").start()
        self.copy(array, own, 26 + zb, "left").start()
        self.copy(array, own, 42 + zb * NX + p.x, "core").start()

    def within(self, z):
        return jnp.logical_and(z >= 0, z <= NZ - 1)

    def onward(self, distance, sign, what):
        p = self.p
        zb = p.z - sign * distance
        for n, child in enumerate(self.tree.get(distance, ())):
            reach = sign * (child - distance)
            slot = 16 + n if distance == 0 and sign < 0 else 8 * n + zb

            @pl.when(self.within(p.z + reach))
            def _(reach=reach, slot=slot):
                for a in range(2):
                    what(a, block_id(zb, p.x, p.k), slot, reach)

    def column(self, distance):
        p = self.p

        def send(a, block, slot, reach):
            self.copy(a, block, slot, reach).start()

        if distance == 0:
            self.onward(0, 1, send)
            self.onward(0, -1, send)
            for a in range(2):
                self.spread(a, p.z)
            return
        for sign in (1, -1):

            @pl.when(self.within(p.z - sign * distance))
            def _(sign=sign):
                zb = p.z - sign * distance
                for a in range(2):
                    self.arrived(a, block_id(zb, p.x, p.k))
                self.onward(distance, sign, send)
                for a in range(2):
                    self.spread(a, zb)

    def act(self, action):
        what, distance = action[0], int(action[1:])
        if what == "z":
            self.column(distance)
        else:
            self.each(distance, self.from_side if what == "x" else self.from_across)

    def each(self, distance, what):
        p = self.p

        @pl.when(p.z - distance >= 0)
        def _():
            what(p.z - distance)

        if distance:

            @pl.when(p.z + distance <= NZ - 1)
            def _():
                what(p.z + distance)

    def from_side(self, zb):
        p = self.p
        left, right = (p.x + NX - 1) % NX, (p.x + 1) % NX
        for x, relayed, way in ((left, 0, "right"), (right, 1, "left")):
            block = block_id(zb, x, p.k)
            for a in range(2):
                self.arrived(a, block)
                if a == relayed:
                    self.copy(a, block, 34 + zb, way).start()
                self.copy(a, block, 42 + zb * NX + x, "core").start()

    def from_across(self, zb):
        p = self.p
        x = (p.x + 2) % NX
        block = block_id(zb, x, p.k)
        for a in range(2):
            self.arrived(a, block)
            self.copy(a, block, 42 + zb * NX + x, "core").start()

    def other_core(self, landed=None):
        p = self.p

        @pl.loop(0, NZ * NX)
        def _(i):
            for a in range(2):
                self.arrived(a, i * 2 + 1 - p.k)
            if landed is not None:
                landed(i)

    def drain(self):
        p = self.p

        @pl.loop(0, NZ)
        def _(zb):
            own = block_id(zb, p.x, p.k)
            for a in range(2):
                self.copy(a, own, 18 + zb, "right").wait_send()
                self.copy(a, own, 26 + zb, "left").wait_send()
                self.copy(a, own, 34 + zb, "left").wait_send()
                for x in range(NX):
                    self.copy(a, own, 42 + zb * NX + x, "core").wait_send()

        def sent(a, block, slot, reach):
            self.copy(a, block, slot, reach).wait_send()

        for distance in self.tree:
            for sign in (1, -1):

                @pl.when(self.within(p.z - sign * distance))
                def _(distance=distance, sign=sign):
                    self.onward(distance, sign, sent)


CHUNKS = 8


class FeatureGather:
    N_SEND = 7 * CHUNKS

    def __init__(self, place, x_ref, buf, send, recv):
        self.p, self.x_ref, self.buf, self.send, self.recv = place, x_ref, buf, send, recv
        self.rows = x_ref.shape[0] // CHUNKS
        p = place
        self.across_z = {"tp": p.y * 2 + 1 - p.h}
        self.right = {"tp": ((p.y + 1) % NY) * 2 + p.h}
        self.left = {"tp": ((p.y + NY - 1) % NY) * 2 + p.h}

    def copy(self, slot, chunk, kind, device, own=False):
        part = pl.ds(chunk * self.rows, self.rows)
        src = self.x_ref.at[part] if own else self.buf.at[slot, part]
        return copy_to(
            src, self.buf.at[slot, part], self.send.at[kind * CHUNKS + chunk], self.recv.at[slot, chunk], device
        )

    def arrived(self, slot, chunk):
        self.copy(slot, chunk, 0, self.left).wait_recv()

    def slots(self, partner):
        p = self.p
        h = 1 - p.h if partner else p.h
        return [((p.y + step) % NY) * 2 + h for step in (0, NY - 1, 1, 2)]

    def act(self, action):
        what = {"y": self.start, "c": self.cross, "r": self.relay, "p": self.partner, "q": self.partner_relay}
        what[action[0]](int(action[1:]))

    def start(self, _):
        own = self.p.tp
        for i in range(CHUNKS):
            self.copy(own, i, 1, self.right, True).start()
            self.copy(own, CHUNKS - 1 - i, 2, self.left, True).start()

    def cross(self, i):
        self.copy(self.p.tp, i, 0, self.across_z, True).start()

    def relay(self, i):
        _, left, right, _ = self.slots(False)
        last = CHUNKS - 1 - i
        self.arrived(left, i)
        if i < CHUNKS // 2:
            self.copy(left, i, 3, self.right).start()
        self.arrived(right, last)
        if i < CHUNKS // 2:
            self.copy(right, last, 3, self.left).start()

    def partner(self, i):
        slot = self.slots(True)[0]
        self.arrived(slot, i)
        self.copy(slot, i, 4, self.right).start()
        self.copy(slot, i, 5, self.left).start()

    def partner_relay(self, i):
        _, left, right, _ = self.slots(True)
        self.arrived(left, i)
        if i % 2 == 0:
            self.copy(left, i, 6, self.right).start()
        self.arrived(right, i)
        if i % 2 == 1:
            self.copy(right, i, 6, self.left).start()

    def across(self, i):
        for partner in (False, True):
            self.arrived(self.slots(partner)[3], i)

    def drain(self):
        for kind in range(7):
            for i in range(CHUNKS):
                self.copy(self.p.tp, i, kind, self.left, True).wait_send()


SCHEDULE = (
    "z0", "y0", "c0", "z1", "x0", "c1", "r0", "r1", "z2", "x1", "a0", "c2", "r2", "r3", "z3", "x2", "a1", "c3", "r4",
    "r5", "z4", "x3", "a2", "c4", "r6", "r7", "z5", "x4", "a3", "c5", "p0", "z6", "x5", "a4", "c6", "p1", "z7", "x6",
    "a5", "c7", "p2", "q0", "x7", "a6", "p3", "q1", "t", "p4", "q2", "n0", "a7", "p5", "q3", "n1", "o", "p6", "q4",
    "n2", "p7", "q5", "n3", "q6", "n4", "q7", "n5", "n6", "n7",
)


def greet(devices, optional):
    barrier = pltpu.get_barrier_semaphore()
    count = len(devices)
    for device in devices:
        pl.semaphore_signal(barrier, inc=1, device_id=device, device_id_type=MESH)
    for there, device in optional:

        @pl.when(there)
        def _(device=device):
            pl.semaphore_signal(barrier, inc=1, device_id=device, device_id_type=MESH)

        count = count + there.astype(jnp.int32)
    pl.semaphore_wait(barrier, count)


def ctx_partners(p):
    fixed = [{"ctx": p.ctx_neighbour(w)} for w in ("right", "left", "core")]
    optional = []
    for reach in REACHES:
        optional.append((p.z + reach <= NZ - 1, {"ctx": p.ctx_neighbour(reach)}))
        optional.append((p.z - reach >= 0, {"ctx": p.ctx_neighbour(-reach)}))
    return fixed, optional


def project_kernel(
    pair_ref, x_ref, gain_ref, wk_ref, wv_ref, freq_ref, keys_ref, values_ref, where_ref,
    xbuf, normed, wk_buf, wv_buf, turn, key_buf, value_buf, w_send, w_recv, x_send, x_recv, kv_send, kv_recv, local, store,
):
    p = Place()
    own = p.ctx
    rows, width = x_ref.shape
    half = rows // 2
    weights = CtxGather(p, LINE, (wk_buf, wv_buf), w_send, w_recv)
    features = FeatureGather(p, x_ref, xbuf, x_send, x_recv)
    spread = CtxGather(p, HUB, (key_buf, value_buf), kv_send, kv_recv)
    copies = [
        pltpu.make_async_copy(wk_ref, wk_buf.at[own, pl.ds(0, 128)], local.at[0]),
        pltpu.make_async_copy(wv_ref, wv_buf.at[own], local.at[1]),
        pltpu.make_async_copy(x_ref, xbuf.at[p.tp], local.at[2]),
    ]
    for c in copies:
        c.start()
    pair = pair_ref[0]
    wk_buf[own, pl.ds(128, EXT), :] = jnp.full((EXT, 128), pair.astype(jnp.float32), jnp.bfloat16)
    fixed, optional = ctx_partners(p)
    greet(fixed + [features.right, features.left, features.across_z], optional)
    for c in copies:
        c.wait()

    def normalize(chunk):
        part = pl.ds(chunk * features.rows, features.rows)
        squares = jnp.zeros((features.rows, HEAD), jnp.float32)
        for f in range(8):
            for i in range(width // HEAD):
                piece = xbuf[f, part, pl.ds(i * HEAD, HEAD)].astype(jnp.float32)
                squares = squares + piece * piece
        inverse = lax.rsqrt(jnp.sum(squares, axis=1, keepdims=True) / (8.0 * width) + EPSILON)
        for f in range(8):
            for i in range(width // HEAD):
                piece = xbuf[f, part, pl.ds(i * HEAD, HEAD)].astype(jnp.float32)
                gain = gain_ref[pl.ds(f * (width // HEAD) + i, 1), :]
                normed[f, part, pl.ds(i * HEAD, HEAD)] = (piece * inverse * gain).astype(jnp.bfloat16)

    token = lax.broadcasted_iota(jnp.int32, (rows, HEAD), 0)
    lane = lax.broadcasted_iota(jnp.int32, (rows, HEAD), 1)
    position = jnp.where(token < half, pair * half + token, (2 * NCTX - 1 - pair) * half + token - half)
    angle = position.astype(jnp.float32) * freq_ref[...]

    for action in SCHEDULE:
        if action[0] in "zxa":
            weights.act(action)
        elif action == "o":
            weights.other_core()
            held = jnp.max(wk_buf[:, pl.ds(128, EXT), :].astype(jnp.float32), axis=1)
            owner = lax.broadcasted_iota(jnp.int32, (NCTX, 128), 0).astype(jnp.float32)
            wanted = lax.broadcasted_iota(jnp.int32, (NCTX, 128), 1).astype(jnp.float32)
            where_ref[...] = jnp.sum(jnp.where(held == wanted, owner, 0.0), axis=0, keepdims=True).astype(jnp.int32)
        elif action == "t":
            turn[0] = jnp.cos(angle)
            turn[1] = jnp.where(lane < HEAD // 2, -jnp.sin(angle), jnp.sin(angle))
        elif action[0] == "n":
            features.across(int(action[1:]))
            normalize(int(action[1:]))
        else:
            features.act(action)

    keys = jnp.zeros((rows, HEAD), jnp.float32)
    values = jnp.zeros((rows, HEAD), jnp.float32)
    for f in range(8):
        wk = wk_buf[pl.ds(f * 8, 8), pl.ds(0, 128), :].reshape(width, HEAD)
        wv = wv_buf[pl.ds(f * 8, 8)].reshape(width, HEAD)
        keys = keys + jnp.dot(normed[f], wk, preferred_element_type=jnp.float32)
        values = values + jnp.dot(normed[f], wv, preferred_element_type=jnp.float32)
    key_buf[own] = (keys * turn[0] + pltpu.roll(keys, HEAD // 2, 1) * turn[1]).astype(jnp.bfloat16)
    value_buf[own] = values.astype(jnp.bfloat16)
    weights.drain()

    for action in SPREAD:
        spread.act(action)

    def stores(i):
        pair_of_blocks = pl.ds(i * 2, 2)
        return (
            pltpu.make_async_copy(key_buf.at[pair_of_blocks], keys_ref.at[pair_of_blocks], store.at[0, i]),
            pltpu.make_async_copy(value_buf.at[pair_of_blocks], values_ref.at[pair_of_blocks], store.at[1, i]),
        )

    def landed(i):
        for c in stores(i):
            c.start()

    spread.other_core(landed)
    features.drain()
    spread.drain()

    @pl.loop(0, NCTX // 2)
    def _(i):
        for c in stores(i):
            c.wait()


SPANS = 4
MOST_SPANS = 36


def attend_kernel(
    pair_ref, docs_ref, where_ref, q_ref, keys_ref, values_ref, out_ref, k_buf, v_buf, all_scores, highest, total, acc, sem
):
    group = q_ref.shape[1] // HEAD
    rows = HALF * group
    wide = SPANS * HALF
    factor = HEAD ** (-0.5) * math.log2(math.e)
    ends = []
    end = jnp.int32(0)
    for d in range(docs_ref.shape[0]):
        end = end + docs_ref[d]
        ends.append(end)
    pair = pair_ref[0]

    def start_of(position):
        first = jnp.zeros_like(position)
        for e in ends:
            first = jnp.where(position >= e, e, first)
        return first

    spans = [pair, 2 * NCTX - 1 - pair]
    firsts = [start_of(span * HALF) // HALF for span in spans]
    groups = [(span - first) // SPANS + 1 for span, first in zip(spans, firsts)]

    def fetches(part, i):
        j = jnp.minimum(firsts[part] + i, spans[part])
        late = j >= NCTX
        holder = where_ref[0, jnp.where(late, 2 * NCTX - 1 - j, j)]
        source = pl.ds(pl.multiple_of(jnp.where(late, HALF, 0), HALF), HALF)
        target = pl.ds(pl.multiple_of(i * HALF, HALF), HALF)
        return (
            pltpu.make_async_copy(keys_ref.at[holder, source], k_buf.at[part, target], sem.at[0, part, i]),
            pltpu.make_async_copy(values_ref.at[holder, source], v_buf.at[part, target], sem.at[1, part, i]),
        )

    for part in range(2):

        @pl.loop(0, groups[part] * SPANS)
        def _(i, part=part):
            for c in fetches(part, i):
                c.start()

    token = lax.broadcasted_iota(jnp.int32, (rows, 1), 0) % HALF
    for part in range(2):
        span, first, count = spans[part], firsts[part], groups[part]
        q = jnp.concatenate(
            [q_ref[pl.ds(part * HALF, HALF), pl.ds(h * HEAD, HEAD)] for h in range(group)], axis=0
        )
        position = span * HALF + token
        start = start_of(position)
        last_start = start_of(span * HALF + HALF - 1)
        highest[...] = jnp.full_like(highest, NEG)

        @pl.loop(0, count)
        def _(g, part=part):
            for i in range(SPANS):
                fetches(part, g * SPANS + i)[0].wait()
            lead = first + g * SPANS
            kk = k_buf[part, pl.ds(pl.multiple_of(g * wide, wide), wide), :]
            scores = lax.dot_general(
                q, kk, (((1,), (1,)), ((), ())), preferred_element_type=jnp.float32
            )
            inside = jnp.logical_and(lead * HALF >= last_start, lead + SPANS <= span)

            @pl.when(inside)
            def _():
                all_scores[g] = scores
                highest[...] = jnp.maximum(highest[...], scores)

            @pl.when(jnp.logical_not(inside))
            def _():
                place = lead * HALF + lax.broadcasted_iota(jnp.int32, (1, wide), 1)
                allowed = jnp.logical_and(place >= start, place <= position)
                masked = jnp.where(allowed, scores, NEG)
                all_scores[g] = masked
                highest[...] = jnp.maximum(highest[...], masked)

        top = jnp.max(highest[...], axis=1, keepdims=True) * factor
        total[...] = jnp.zeros_like(total)
        acc[...] = jnp.zeros_like(acc)

        @pl.loop(0, count)
        def _(g, part=part):
            for i in range(SPANS):
                fetches(part, g * SPANS + i)[1].wait()
            weights = jnp.exp2(all_scores[g] * factor - top)
            partial = weights[:, :HEAD]
            for i in range(1, wide // HEAD):
                partial = partial + weights[:, i * HEAD : (i + 1) * HEAD]
            total[...] += partial
            acc[...] += jnp.dot(
                weights.astype(jnp.bfloat16),
                v_buf[part, pl.ds(pl.multiple_of(g * wide, wide), wide), :],
                preferred_element_type=jnp.float32,
            )

        done = (acc[...] / jnp.sum(total[...], axis=1, keepdims=True)).astype(jnp.bfloat16)
        for h in range(group):
            out_ref[pl.ds(part * HALF, HALF), pl.ds(h * HEAD, HEAD)] = done[h * HALF : (h + 1) * HALF]


def shards(hidden_x, norm_gain, key_projection, value_projection, queries, span_pair, doc_lengths):
    rows, width = hidden_x.shape
    vmem, smem, anywhere = (
        pl.BlockSpec(memory_space=pltpu.VMEM),
        pl.BlockSpec(memory_space=pltpu.SMEM),
        pl.BlockSpec(memory_space=pl.ANY),
    )
    bf16 = jnp.bfloat16
    exponents = np.arange(HEAD // 2, dtype=np.float32) * np.float32(2.0 / HEAD)
    frequency = np.power(np.float64(ROPE_BASE), -exponents.astype(np.float64)).astype(np.float32)
    frequency = jnp.asarray(np.concatenate([frequency, frequency])[None])
    dma = pltpu.SemaphoreType.DMA
    keys, values, where = pl.pallas_call(
        project_kernel,
        out_shape=(
            jax.ShapeDtypeStruct((NCTX, rows, HEAD), bf16),
            jax.ShapeDtypeStruct((NCTX, rows, HEAD), bf16),
            jax.ShapeDtypeStruct((1, 128), jnp.int32),
        ),
        in_specs=[smem, anywhere, vmem, anywhere, anywhere, vmem],
        out_specs=(anywhere, anywhere, vmem),
        scratch_shapes=[
            pltpu.VMEM((8, rows, width), bf16),
            pltpu.VMEM((8, rows, width), bf16),
            pltpu.VMEM((NCTX, 128 + EXT, HEAD), bf16),
            pltpu.VMEM((NCTX, 128, HEAD), bf16),
            pltpu.VMEM((2, rows, HEAD), jnp.float32),
            pltpu.VMEM((NCTX, rows, HEAD), bf16),
            pltpu.VMEM((NCTX, rows, HEAD), bf16),
            dma((2, CtxGather.N_SEND)),
            dma((2, NCTX)),
            dma((FeatureGather.N_SEND,)),
            dma((8, CHUNKS)),
            dma((2, CtxGather.N_SEND)),
            dma((2, NCTX)),
            dma((3,)),
            dma((2, NCTX // 2)),
        ],
        compiler_params=pltpu.CompilerParams(
            collective_id=0, has_side_effects=True, vmem_limit_bytes=VMEM_LIMIT
        ),
        name="project",
    )(
        span_pair,
        hidden_x,
        norm_gain.reshape(8 * width // HEAD, HEAD),
        key_projection,
        value_projection,
        frequency,
    )
    group = queries.shape[1] // HEAD
    return pl.pallas_call(
        attend_kernel,
        out_shape=jax.ShapeDtypeStruct(queries.shape, bf16),
        in_specs=[smem, smem, smem, vmem, anywhere, anywhere],
        out_specs=vmem,
        scratch_shapes=[
            pltpu.VMEM((2, MOST_SPANS * HALF, HEAD), bf16),
            pltpu.VMEM((2, MOST_SPANS * HALF, HEAD), bf16),
            pltpu.VMEM((MOST_SPANS // SPANS, HALF * group, SPANS * HALF), jnp.float32),
            pltpu.VMEM((HALF * group, SPANS * HALF), jnp.float32),
            pltpu.VMEM((HALF * group, HEAD), jnp.float32),
            pltpu.VMEM((HALF * group, HEAD), jnp.float32),
            dma((2, 2, MOST_SPANS)),
        ],
        compiler_params=pltpu.CompilerParams(vmem_limit_bytes=VMEM_LIMIT),
        name="attend",
    )(span_pair, doc_lengths, where, queries, keys, values)


def solution(mesh):
    placed = (P("ctx", "tp"), P(), P("ctx", "tp"), P("ctx", "tp"), P("ctx", "tp"), P("ctx"), P())
    return jax.shard_map(
        shards, mesh=mesh, in_specs=placed, out_specs=P("ctx", "tp"), check_vma=False
    )
```
